32 devices in a mesh: fsdp: 32 (over z, y, x, core).
Axes of the slice: x: 2, y: 2, z: 4, core: 2. Of those that a mesh axis runs over, the one named last changes fastest.
Arguments:
- inputs: bfloat16 [4096, 1024], P('fsdp'), may hold values from -6 to 6
- cotangent: bfloat16 [4096, 1024], P('fsdp'), may hold values from -6 to 6
- sequence_ids: int32 [4096], P('fsdp'), may hold values from -1 to 4095, as said below
- positions: int32 [4096], P('fsdp'), may hold values from 0 to 2047, as said below
- attend_weight: bfloat16 [3145728], P('fsdp'), may hold values from -0.1875 to 0.1875
- output_weight: bfloat16 [1048576], P('fsdp'), may hold values from -0.5 to 0.5
- expand_weight: bfloat16 [4194304], P('fsdp'), may hold values from -0.1875 to 0.1875
- reduce_weight: bfloat16 [4194304], P('fsdp'), may hold values from -0.09375 to 0.09375
- small_params: bfloat16 [13312], P('fsdp'), may hold values from -3 to 3
Outputs:
- layer_out: bfloat16 [4096, 1024], P('fsdp')
- input_grad: float32 [4096, 1024], P('fsdp')
- attend_grad: float32 [3145728], P('fsdp')
- output_grad: float32 [1048576], P('fsdp')
- expand_grad: float32 [4194304], P('fsdp')
- reduce_grad: float32 [4194304], P('fsdp')
- small_grad: float32 [13312], P('fsdp')
The draws below stay inside these ranges and needn't reach their ends.
Inputs may be any that keep to these rules, and one draw needn't show every extreme that they name: `sequence_ids`: the rows of one device hold whole sequences one after another, then empty rows marked -1; no sequence lies on two devices; some device has no empty row. Within a sequence positions rise by one from row to row; empty rows hold 0.
All inputs are finite; a program needn't handle non-finite values.
Results may differ from the reference program's by a relative error of at most 0.009.
Values may be sent and summed in bfloat16 or wider, within the bound.
A program may use at most 128 MiB of HBM per device.

```python
import math
import jax
import jax.numpy as jnp
from jax import lax

H = 16
HD = 64
D = 1024
ROT = 16
FF = 4096
CAP = 128
MAXPOS = 2048
TOKENS = 4096
N_FSDP = 32


def layout(key):
    base = jax.random.fold_in(key, 17)
    keyset = jax.random.split(base, 5)
    device_count = TOKENS // CAP
    order = jnp.arange(CAP, dtype=jnp.int32)[None, :]
    partial_fill = jax.random.randint(keyset[0], (device_count,), CAP // 8 + 1, 5 * CAP // 8 + 1)
    crowded = jax.random.randint(keyset[1], (device_count,), 0, 8) == 0
    fullest = jax.random.randint(keyset[2], (), 0, device_count)
    crowded = crowded | (jnp.arange(device_count) == fullest)
    filled = jnp.where(crowded, CAP, partial_fill)
    occupied = order < filled[:, None]
    coins = jax.random.randint(keyset[3], (device_count, CAP), 0, 24) == 0
    starts = occupied & ((order == 0) | coins)
    local_index = jnp.cumsum(starts.astype(jnp.int32), axis=1) - 1
    owner = jnp.arange(device_count, dtype=jnp.int32)[:, None] * CAP
    sequence = jnp.where(occupied, owner + local_index, -1)
    first_row = lax.cummax(jnp.where(starts, order, 0), axis=1)
    offsets = jax.random.randint(keyset[4], (device_count, CAP), 0, MAXPOS - CAP + 1)
    start_at = jnp.take_along_axis(offsets, first_row, axis=1)
    placed = jnp.where(occupied, start_at + order - first_row, 0)
    return (sequence.reshape(TOKENS).astype(jnp.int32), placed.reshape(TOKENS).astype(jnp.int32))


def draw_sequence_ids(key, part):
    return layout(key)[0]


def draw_positions(key, part):
    return layout(key)[1]


def spread_piece(piece_key, count, spread):
    return spread * jax.random.normal(piece_key, (count,), jnp.float32)


def gain_piece(piece_key):
    return jax.random.uniform(piece_key, (D,), jnp.float32, 0.5, 1.5)


def attend_bias_piece(piece_key):
    return 0.5 * jax.random.normal(piece_key, (3 * D,), jnp.float32)


def draw_small_params(key, part):
    keyset = jax.random.split(jax.random.fold_in(key, 29), 8)
    pieces = [gain_piece(keyset[0]), spread_piece(keyset[1], D, 0.3), gain_piece(keyset[2]), spread_piece(keyset[3], D, 0.3), attend_bias_piece(keyset[4]), spread_piece(keyset[5], D, 0.3), spread_piece(keyset[6], FF, 0.5), spread_piece(keyset[7], D, 0.3)]
    return jnp.clip(jnp.concatenate(pieces), -3.0, 3.0).astype(jnp.bfloat16)


def block_scale(rng, dims, cuts, least, top_value):
    loudness, own = 1.0, jax.random.fold_in(rng, 6)
    for axis_at, blocks in cuts:
        steps = jnp.exp(jax.random.uniform(jax.random.fold_in(own, axis_at), (blocks,), jnp.float32, least / len(cuts), top_value / len(cuts)))
        loudness = loudness * jnp.repeat(steps, dims[axis_at] // blocks).reshape([-1 if axis == axis_at else 1 for axis in range(len(dims))])
    return loudness


def normal_values(rng, dims, width, reach, cuts=(), kind=jnp.bfloat16):
    result = width * jax.random.normal(rng, dims, jnp.float32)
    if cuts:
        result = result * block_scale(rng, dims, cuts, -0.22, 0.18)
    return jnp.clip(result, -reach, reach).astype(kind)


def setup_inputs(seed: int = 0) -> dict:
    splits = jax.random.split(jax.random.key(seed), 10)
    inputs = normal_values(splits[0], (TOKENS, D), 1.0, 6.0, ((0, 32),))
    cotangent = normal_values(splits[1], (TOKENS, D), 1.0, 6.0, ((0, 32),))
    sequence_ids = draw_sequence_ids(jax.random.fold_in(splits[9], 71), 0)
    positions = draw_positions(jax.random.fold_in(splits[9], 71), 0)
    attend_weight = normal_values(splits[4], (3 * D * D,), D ** -0.5, 0.1875, ((0, 32),))
    output_weight = normal_values(splits[5], (D * D,), (D // 8) ** -0.5, 0.5, ((0, 32),))
    expand_weight = normal_values(splits[6], (D * FF,), D ** -0.5, 0.1875, ((0, 32),))
    reduce_weight = normal_values(splits[7], (FF * D,), FF ** -0.5, 0.09375, ((0, 32),))
    small_params = draw_small_params(jax.random.fold_in(splits[9], 71), 0)
    return dict(inputs=inputs, cotangent=cotangent, sequence_ids=sequence_ids, positions=positions, attend_weight=attend_weight, output_weight=output_weight, expand_weight=expand_weight, reduce_weight=reduce_weight, small_params=small_params)


norm_epsilon = 1e-05
masked_score = -1e+30

def left_product(former, latter):
    return lax.dot_general(former, latter, (((0,), (0,)), ((), ())), preferred_element_type=jnp.float32)

def right_product(former, latter):
    return lax.dot_general(former, latter, (((1,), (1,)), ((), ())), preferred_element_type=jnp.float32)

def batched(form, former, latter):
    return jnp.einsum(form, former.astype(jnp.float32), latter.astype(jnp.float32))

def layer_norm(values, gain, shift):
    center = values - lax.optimization_barrier(jnp.mean(values, axis=-1, keepdims=True))
    spread = lax.optimization_barrier(jnp.mean(center * center, axis=-1, keepdims=True))
    return center * lax.rsqrt(spread + norm_epsilon) * gain + shift

def rotary_tables(positions):
    halfway = ROT // 2
    powers = jnp.arange(halfway, dtype=jnp.float32) * (2.0 / ROT)
    inverse = 10000.0 ** (-powers)
    angles = positions.astype(jnp.float32)[:, None] * inverse[None, :]
    return (jnp.cos(angles)[:, None, :], jnp.sin(angles)[:, None, :])

def rotate(values, cosine, sine, direction):
    halfway = ROT // 2
    leading = values[..., :halfway]
    trailing = values[..., halfway:ROT]
    new_leading = leading * cosine - direction * trailing * sine
    new_trailing = trailing * cosine + direction * leading * sine
    return jnp.concatenate([new_leading, new_trailing, values[..., ROT:]], axis=-1)

def allowed_pairs(sequence):
    row_order = jnp.arange(sequence.shape[0])
    return (sequence[:, None] == sequence[None, :]) & (row_order[None, :] <= row_order[:, None])

def unpack(attend_flat, output_flat, expand_flat, reduce_flat, small_flat):
    widened = small_flat.astype(jnp.float32)
    return (attend_flat.reshape(3 * D, D), output_flat.reshape(D, D), expand_flat.reshape(FF, D), reduce_flat.reshape(FF, D), widened[0:D], widened[D:2 * D], widened[2 * D:3 * D], widened[3 * D:4 * D], widened[4 * D:7 * D], widened[7 * D:8 * D], widened[8 * D:8 * D + FF], widened[8 * D + FF:9 * D + FF])

def attention_scores(query_heads, key_heads, sequence):
    scale_factor = 1.0 / math.sqrt(HD)
    scores = batched('qhd,khd->hqk', query_heads, key_heads) * scale_factor
    return jnp.where(allowed_pairs(sequence)[None], scores, masked_score)

def forward(inputs, sequence, positions, params):
    weight_attend, weight_output, weight_expand, weight_reduce, gain_one, shift_one, gain_two, shift_two, bias_attend, bias_output, bias_expand, bias_reduce = params
    row_count = inputs.shape[0]
    wide_input = inputs.astype(jnp.float32)
    normed_one = layer_norm(wide_input, gain_one, shift_one).astype(jnp.bfloat16)
    normed_two = layer_norm(wide_input, gain_two, shift_two).astype(jnp.bfloat16)
    projected = right_product(normed_one, weight_attend) + bias_attend
    split = projected.reshape(row_count, H, 3, HD)
    cosine, sine = rotary_tables(positions)
    query_heads = rotate(split[:, :, 0], cosine, sine, 1.0).astype(jnp.bfloat16)
    key_heads = rotate(split[:, :, 1], cosine, sine, 1.0).astype(jnp.bfloat16)
    value_heads = split[:, :, 2].astype(jnp.bfloat16)
    scores = attention_scores(query_heads, key_heads, sequence)
    highest = lax.optimization_barrier(jnp.max(scores, axis=-1, keepdims=True))
    raised = jnp.exp(scores - highest)
    totals = lax.optimization_barrier(jnp.sum(raised, axis=-1, keepdims=True))
    soft_low = (raised / totals).astype(jnp.bfloat16)
    log_total = highest + jnp.log(totals)
    mixed_heads = batched('hqk,khd->qhd', soft_low, value_heads).astype(jnp.bfloat16).reshape(row_count, D)
    attended = jnp.dot(mixed_heads, weight_output, preferred_element_type=jnp.float32) + bias_output
    expanded = right_product(normed_two, weight_expand) + bias_expand
    activated = jax.nn.gelu(expanded, approximate=False).astype(jnp.bfloat16)
    reduced = jnp.dot(activated, weight_reduce, preferred_element_type=jnp.float32) + bias_reduce
    layer_out = (wide_input + attended + reduced).astype(jnp.bfloat16)
    stored = (normed_one, normed_two, query_heads, key_heads, value_heads, log_total, mixed_heads, expanded, activated, cosine, sine)
    return (layer_out, stored)

def exact_gelu(values):
    return jax.nn.gelu(values, approximate=False)

def feed_backward(cotangent, sequence, params, stored):
    weight_expand, weight_reduce = (params[2], params[3])
    normed_two, expanded, activated = (stored[1], stored[7], stored[8])
    occupied = (sequence >= 0)[:, None]
    grad_out = jnp.where(occupied, cotangent, jnp.zeros_like(cotangent))
    wide_grad = grad_out.astype(jnp.float32)
    grad_reduce = left_product(activated, grad_out)
    grad_bias_reduce = lax.optimization_barrier(jnp.sum(wide_grad, axis=0))
    grad_activated = right_product(grad_out, weight_reduce)
    pullback = jax.vjp(exact_gelu, expanded)[1]
    grad_expanded = pullback(grad_activated)[0].astype(jnp.bfloat16)
    grad_expand = left_product(grad_expanded, normed_two)
    grad_bias_expand = lax.optimization_barrier(jnp.sum(grad_expanded.astype(jnp.float32), axis=0))
    grad_normed_two = jnp.dot(grad_expanded, weight_expand, preferred_element_type=jnp.float32)
    return (grad_out, (grad_expand, grad_reduce), (grad_bias_expand, grad_bias_reduce, grad_normed_two))

def attend_backward(inputs, grad_out, sequence, params, stored, feed_small):
    weight_attend, weight_output, weight_expand, weight_reduce, gain_one, shift_one, gain_two, shift_two, bias_attend, bias_output, bias_expand, bias_reduce = params
    normed_one, normed_two, query_heads, key_heads, value_heads, log_total, mixed_heads, expanded, activated, cosine, sine = stored
    grad_bias_expand, grad_bias_reduce, grad_normed_two = feed_small
    row_count = inputs.shape[0]
    scale_factor = 1.0 / math.sqrt(HD)
    wide_grad = grad_out.astype(jnp.float32)
    grad_output = left_product(mixed_heads, grad_out)
    grad_bias_output = lax.optimization_barrier(jnp.sum(wide_grad, axis=0))
    grad_mixed = right_product(grad_out, weight_output).astype(jnp.bfloat16).reshape(row_count, H, HD)
    scores = attention_scores(query_heads, key_heads, sequence)
    recomputed = jnp.exp(scores - log_total)
    grad_soft = batched('qhd,khd->hqk', grad_mixed, value_heads)
    row_inner = lax.optimization_barrier(jnp.sum(recomputed * grad_soft, axis=-1, keepdims=True))
    grad_scores = (recomputed * (grad_soft - row_inner) * scale_factor).astype(jnp.bfloat16)
    grad_values = batched('hqk,qhd->khd', recomputed.astype(jnp.bfloat16), grad_mixed)
    grad_queries = rotate(batched('hqk,khd->qhd', grad_scores, key_heads), cosine, sine, -1.0)
    grad_keys = rotate(batched('hqk,qhd->khd', grad_scores, query_heads), cosine, sine, -1.0)
    grad_projected = jnp.stack([grad_queries, grad_keys, grad_values], axis=2).reshape(row_count, 3 * D).astype(jnp.bfloat16)
    grad_attend = left_product(grad_projected, normed_one)
    grad_bias_attend = lax.optimization_barrier(jnp.sum(grad_projected.astype(jnp.float32), axis=0))
    grad_normed_one = jnp.dot(grad_projected, weight_attend, preferred_element_type=jnp.float32)
    wide_input = inputs.astype(jnp.float32)
    pull_one = jax.vjp(layer_norm, wide_input, gain_one, shift_one)[1]
    input_one, grad_gain_one, grad_shift_one = pull_one(grad_normed_one)
    pull_two = jax.vjp(layer_norm, wide_input, gain_two, shift_two)[1]
    input_two, grad_gain_two, grad_shift_two = pull_two(grad_normed_two)
    input_grad = wide_grad + input_one + input_two
    small_grad = jnp.concatenate([grad_gain_one, grad_shift_one, grad_gain_two, grad_shift_two, grad_bias_attend, grad_bias_output, grad_bias_expand, grad_bias_reduce])
    return (input_grad, (grad_attend, grad_output, small_grad))

def reference(inputs, cotangent, sequence_ids, positions, attend_weight, output_weight, expand_weight, reduce_weight, small_params):
    params = unpack(attend_weight, output_weight, expand_weight, reduce_weight, small_params)
    sections = (inputs.reshape(N_FSDP, CAP, D), cotangent.reshape(N_FSDP, CAP, D), sequence_ids.reshape(N_FSDP, CAP), positions.reshape(N_FSDP, CAP))

    def through_block(running, section):
        block_input, block_cotangent, block_sequence, block_positions = section
        layer_out, stored = forward(block_input, block_sequence, block_positions, params)
        grad_out, feed_mats, feed_small = feed_backward(block_cotangent, block_sequence, params, stored)
        input_grad, others = attend_backward(block_input, grad_out, block_sequence, params, stored, feed_small)
        pieces = (others[0].reshape(-1), others[1].reshape(-1), feed_mats[0].reshape(-1), feed_mats[1].reshape(-1), others[2])
        updated = tuple((total + piece for total, piece in zip(running, pieces)))
        return (updated, (layer_out, input_grad))
    starting = (jnp.zeros((3 * D * D,), jnp.float32), jnp.zeros((D * D,), jnp.float32), jnp.zeros((D * FF,), jnp.float32), jnp.zeros((FF * D,), jnp.float32), jnp.zeros((9 * D + FF,), jnp.float32))
    totals, stacked = lax.scan(through_block, starting, sections)
    layer_out = stacked[0].reshape(TOKENS, D)
    input_grad = stacked[1].reshape(TOKENS, D)
    return (layer_out, input_grad, totals[0], totals[1], totals[2], totals[3], totals[4])
```

```python
import math

import jax
import jax.numpy as jnp
from jax import lax
from jax.sharding import PartitionSpec as P

H = 16
HD = 64
D = 1024
ROT = 16
FF = 4096


norm_epsilon = 1e-05
masked_score = -1e30


def swap(block, mask):
    count = lax.axis_size("fsdp")
    return lax.ppermute(block, "fsdp", [(place, place ^ mask) for place in range(count)])


def left_product(former, latter):
    return lax.dot_general(
        former, latter, (((0,), (0,)), ((), ())), preferred_element_type=jnp.float32
    )


def right_product(former, latter):
    return lax.dot_general(
        former, latter, (((1,), (1,)), ((), ())), preferred_element_type=jnp.float32
    )


def batched(form, former, latter):
    return jnp.einsum(form, former, latter, preferred_element_type=jnp.float32)


def layer_norm(values, gain, shift):
    center = values - jnp.mean(values, axis=-1, keepdims=True)
    spread = jnp.mean(center * center, axis=-1, keepdims=True)
    return center * lax.rsqrt(spread + norm_epsilon) * gain + shift


def rotary_tables(positions):
    halfway = ROT // 2
    powers = jnp.arange(halfway, dtype=jnp.float32) * (2.0 / ROT)
    inverse = 10000.0 ** (-powers)
    angles = positions.astype(jnp.float32)[:, None] * inverse[None, :]
    return (jnp.cos(angles)[:, None, :], jnp.sin(angles)[:, None, :])


def rotate(values, cosine, sine, direction):
    halfway = ROT // 2
    leading = values[..., :halfway]
    trailing = values[..., halfway:ROT]
    new_leading = leading * cosine - direction * trailing * sine
    new_trailing = trailing * cosine + direction * leading * sine
    return jnp.concatenate([new_leading, new_trailing, values[..., ROT:]], axis=-1)


def exact_gelu(values):
    return jax.nn.gelu(values, approximate=False)


def norm_pair(wide_input, norms):
    normed_one = layer_norm(wide_input, norms[0], norms[1]).astype(jnp.bfloat16)
    normed_two = layer_norm(wide_input, norms[2], norms[3]).astype(jnp.bfloat16)
    return (normed_one, normed_two)


def block_scores(query_blocks, key_blocks, label_blocks):
    scale_factor = 1.0 / math.sqrt(HD)
    scores = batched("bqhd,bkhd->bhqk", query_blocks, key_blocks) * scale_factor
    block_rows = label_blocks.shape[1]
    row_order = jnp.arange(block_rows)
    allowed = (label_blocks[:, :, None] == label_blocks[:, None, :]) & (
        row_order[None, None, :] <= row_order[None, :, None]
    )
    return jnp.where(allowed[:, None], scores, masked_score)


def forward_local(normed_one, normed_two, labels, places, weights, blocks):
    attend_rows, attend_bias, output_rows, expand_rows, expand_bias, reduce_rows = weights
    row_count = normed_one.shape[0]
    heads_here = output_rows.shape[0] // HD
    block_rows = row_count // blocks
    projected = right_product(normed_one, attend_rows) + attend_bias
    split = projected.reshape(row_count, heads_here, 3, HD)
    cosine, sine = rotary_tables(places)
    query_heads = (
        rotate(split[:, :, 0], cosine, sine, 1.0)
        .astype(jnp.bfloat16)
        .reshape(blocks, block_rows, heads_here, HD)
    )
    key_heads = (
        rotate(split[:, :, 1], cosine, sine, 1.0)
        .astype(jnp.bfloat16)
        .reshape(blocks, block_rows, heads_here, HD)
    )
    value_heads = split[:, :, 2].astype(jnp.bfloat16).reshape(blocks, block_rows, heads_here, HD)
    label_blocks = labels.reshape(blocks, block_rows)
    scores = block_scores(query_heads, key_heads, label_blocks)
    highest = jnp.max(scores, axis=-1, keepdims=True)
    raised = jnp.exp(scores - highest)
    totals = jnp.sum(raised, axis=-1, keepdims=True)
    soft_low = (raised / totals).astype(jnp.bfloat16)
    log_total = highest + jnp.log(totals)
    mixed_heads = (
        batched("bhqk,bkhd->bqhd", soft_low, value_heads)
        .astype(jnp.bfloat16)
        .reshape(row_count, heads_here * HD)
    )
    expanded = right_product(normed_two, expand_rows) + expand_bias
    activated = exact_gelu(expanded).astype(jnp.bfloat16)
    partial_value = jnp.dot(mixed_heads, output_rows, preferred_element_type=jnp.float32) + jnp.dot(
        activated, reduce_rows, preferred_element_type=jnp.float32
    )
    stored = (
        normed_one,
        normed_two,
        query_heads,
        key_heads,
        value_heads,
        label_blocks,
        log_total,
        mixed_heads,
        expanded,
        activated,
        cosine,
        sine,
    )
    return (partial_value, stored)


def backward_local(grad_out, stored, weights):
    attend_rows, attend_bias, output_rows, expand_rows, expand_bias, reduce_rows = weights
    (
        normed_one,
        normed_two,
        query_heads,
        key_heads,
        value_heads,
        label_blocks,
        log_total,
        mixed_heads,
        expanded,
        activated,
        cosine,
        sine,
    ) = stored
    blocks, block_rows, heads_here = (
        query_heads.shape[0],
        query_heads.shape[1],
        query_heads.shape[2],
    )
    row_count = grad_out.shape[0]
    scale_factor = 1.0 / math.sqrt(HD)
    grad_reduce = left_product(activated, grad_out)
    grad_activated = right_product(grad_out, reduce_rows)
    pullback = jax.vjp(exact_gelu, expanded)[1]
    grad_expanded = pullback(grad_activated)[0].astype(jnp.bfloat16)
    grad_expand = left_product(grad_expanded, normed_two)
    grad_bias_expand = jnp.sum(grad_expanded.astype(jnp.float32), axis=0)
    grad_normed_two = jnp.dot(grad_expanded, expand_rows, preferred_element_type=jnp.float32)
    grad_output = left_product(mixed_heads, grad_out)
    grad_mixed = (
        right_product(grad_out, output_rows)
        .astype(jnp.bfloat16)
        .reshape(blocks, block_rows, heads_here, HD)
    )
    scores = block_scores(query_heads, key_heads, label_blocks)
    recomputed = jnp.exp(scores - log_total)
    grad_soft = batched("bqhd,bkhd->bhqk", grad_mixed, value_heads)
    row_inner = jnp.sum(recomputed * grad_soft, axis=-1, keepdims=True)
    grad_scores = (recomputed * (grad_soft - row_inner) * scale_factor).astype(jnp.bfloat16)
    grad_values = batched("bhqk,bqhd->bkhd", recomputed.astype(jnp.bfloat16), grad_mixed)
    grad_queries = rotate(
        batched("bhqk,bkhd->bqhd", grad_scores, key_heads).reshape(row_count, heads_here, HD),
        cosine,
        sine,
        -1.0,
    )
    grad_keys = rotate(
        batched("bhqk,bqhd->bkhd", grad_scores, query_heads).reshape(row_count, heads_here, HD),
        cosine,
        sine,
        -1.0,
    )
    grad_projected = (
        jnp.stack([grad_queries, grad_keys, grad_values.reshape(row_count, heads_here, HD)], axis=2)
        .reshape(row_count, 3 * heads_here * HD)
        .astype(jnp.bfloat16)
    )
    grad_attend = left_product(grad_projected, normed_one)
    grad_bias_attend = jnp.sum(grad_projected.astype(jnp.float32), axis=0)
    grad_normed_one = jnp.dot(grad_projected, attend_rows, preferred_element_type=jnp.float32)
    return (
        (grad_attend, grad_output, grad_expand, grad_reduce),
        (grad_bias_attend, grad_bias_expand),
        (grad_normed_one, grad_normed_two),
    )


def double_up(current, levels, device_place):
    for level in levels:
        theirs = swap(current, 1 << level)
        lower = (device_place >> level) % 2 == 0
        leading = jnp.where(lower, current, theirs)
        trailing = jnp.where(lower, theirs, current)
        current = jnp.concatenate([leading, trailing], axis=0)
    return current


def halve_down(total, levels, device_place):
    for level in reversed(levels):
        middle = total.shape[0] // 2
        lower = (device_place >> level) % 2 == 0
        retained = jnp.where(lower, total[:middle], total[middle:])
        outgoing = jnp.where(lower, total[middle:], total[:middle])
        total = retained + swap(outgoing, 1 << level)
    return total


def gather_pieces(piece, count, shift):
    return [piece] + [swap(piece, k << shift) for k in range(1, count)]


def scatter_pieces(pieces, shift):
    total = pieces[0].astype(jnp.float32)
    for k in range(1, len(pieces)):
        total = total + swap(pieces[k].astype(jnp.bfloat16), k << shift).astype(jnp.float32)
    return total


def order_low(stacked, bits, place):
    for bit in range(bits):
        shape = stacked.shape
        pairs = stacked.reshape((shape[0] >> (bit + 1), 2, 1 << bit) + shape[1:])
        flipped = jnp.concatenate([pairs[:, 1:], pairs[:, :1]], axis=1)
        stacked = jnp.where((place >> bit) % 2 == 1, flipped, pairs).reshape(shape)
    return stacked


def gather_rows(block, shift):
    mine = jnp.concatenate(gather_pieces(block, 4, shift), axis=0)
    return jnp.concatenate([mine, swap(mine, 1)], axis=0)


def scatter_rows(partial, shift):
    half = partial.shape[0] // 2
    rows = half // 4
    chip = partial[:half] + swap(partial[half:].astype(jnp.bfloat16), 1).astype(jnp.float32)
    return scatter_pieces([chip[k * rows : (k + 1) * rows] for k in range(4)], shift)


def per_device(
    inputs,
    cotangent,
    sequence_ids,
    positions,
    attend_weight,
    output_weight,
    expand_weight,
    reduce_weight,
    small_params,
):
    count = lax.axis_size("fsdp")
    bits = count.bit_length() - 1
    place = lax.axis_index("fsdp")
    token_shift = bits - 2
    chips = count // 8
    core = place % 2
    chip = (place // 2) % chips
    outer = place // (2 * chips)
    per_head = chips // 4
    head_bits = per_head.bit_length() - 1
    row_count = inputs.shape[0]

    head_wide = attend_weight.shape[0] // D
    out_wide = output_weight.shape[0] // D
    feed_wide = expand_weight.shape[0] // D

    labels_all = gather_rows(jnp.stack([sequence_ids, positions], axis=1), token_shift)
    rows_all = gather_rows(inputs, token_shift)
    attend_own = jnp.concatenate(
        [attend_weight.reshape(head_wide, D), output_weight.reshape(out_wide, D)], axis=0
    )
    attend_half = jnp.stack(gather_pieces(attend_own, chips, 1))
    low, high = attend_half[: chips // 2], attend_half[chips // 2 :]
    kept = jnp.where(core == 0, low, high)
    theirs = swap(jnp.where(core == 0, high, low), 1)
    first = jnp.where(core == 0, kept, theirs)
    second = jnp.where(core == 0, theirs, kept)
    both = order_low(jnp.stack([first, second], axis=1), head_bits, chip)
    attend_rows = both[:, :, :head_wide].reshape(-1, D)
    output_rows = both[:, :, head_wide:].reshape(-1, D)

    small_wide = (
        double_up(small_params[None, :], list(range(bits)), place).reshape(-1).astype(jnp.float32)
    )
    norms = [small_wide[k * D : (k + 1) * D] for k in range(4)]
    heads = [4 * outer + ((2 * core + k) ^ (chip // per_head)) for k in range(2)]
    attend_bias = jnp.concatenate(
        [lax.dynamic_slice_in_dim(small_wide, 4 * D + head * 3 * HD, 3 * HD) for head in heads]
    )
    feeders = [outer * 2 * chips + (chip ^ k) * 2 + core for k in range(chips)]
    expand_bias = jnp.concatenate(
        [
            lax.dynamic_slice_in_dim(small_wide, 8 * D + feeder * feed_wide, feed_wide)
            for feeder in feeders
        ]
    )
    feed_own = jnp.concatenate(
        [expand_weight.reshape(feed_wide, D), reduce_weight.reshape(feed_wide, D)], axis=0
    )
    feed_all = jnp.stack(gather_pieces(feed_own, chips, 1))
    expand_rows = feed_all[:, :feed_wide].reshape(-1, D)
    reduce_rows = feed_all[:, feed_wide:].reshape(-1, D)
    weights = (attend_rows, attend_bias, output_rows, expand_rows, expand_bias, reduce_rows)
    grad_rows = gather_rows(cotangent, token_shift)

    blocks = 8
    wide_all = rows_all.astype(jnp.float32)
    center = wide_all - jnp.mean(wide_all, axis=-1, keepdims=True)
    inverse = lax.rsqrt(jnp.mean(center * center, axis=-1, keepdims=True) + norm_epsilon)
    hat = center * inverse
    normed_one = (hat * norms[0] + norms[1]).astype(jnp.bfloat16)
    normed_two = (hat * norms[2] + norms[3]).astype(jnp.bfloat16)
    partial_value, stored = forward_local(
        normed_one, normed_two, labels_all[:, 0], labels_all[:, 1], weights, blocks
    )
    summed = scatter_rows(partial_value, token_shift)
    wide_input = inputs.astype(jnp.float32)
    layer_out = (
        wide_input + summed + small_wide[7 * D : 8 * D] + small_wide[8 * D + FF : 9 * D + FF]
    ).astype(jnp.bfloat16)

    grad_all = jnp.where((labels_all[:, 0] >= 0)[:, None], grad_rows, jnp.zeros_like(grad_rows))
    mats, bias_parts, norm_parts = backward_local(grad_all, stored, weights)
    grad_attend, grad_output, grad_expand, grad_reduce = mats
    grad_one, grad_two = norm_parts
    norm_total = scatter_rows(grad_one * norms[0] + grad_two * norms[2], token_shift)
    feed_pieces = jnp.concatenate(
        [grad_expand.reshape(chips, feed_wide, D), grad_reduce.reshape(chips, feed_wide, D)], axis=1
    )
    feed_shard = scatter_pieces([feed_pieces[k] for k in range(chips)], 1)
    pairs = jnp.concatenate(
        [
            grad_attend.reshape(chips // 2, 2, head_wide, D),
            grad_output.reshape(chips // 2, 2, out_wide, D),
        ],
        axis=2,
    )
    pairs = order_low(pairs, head_bits, chip)
    kept = jnp.where(core == 0, pairs[:, 0], pairs[:, 1])
    theirs = swap(
        jnp.where(core == 0, pairs[:, 1], pairs[:, 0]).astype(jnp.bfloat16), 1
    ).astype(jnp.float32)
    low = jnp.where(core == 0, kept, theirs)
    high = jnp.where(core == 0, theirs, kept)
    halves = [low[k] for k in range(chips // 2)] + [high[k] for k in range(chips // 2)]
    attend_shard = scatter_pieces(halves, 1)

    grad_out = jnp.where((sequence_ids >= 0)[:, None], cotangent, jnp.zeros_like(cotangent))
    wide_grad = grad_out.astype(jnp.float32)
    own_hat = hat[:row_count]
    input_grad = wide_grad + inverse[:row_count] * (
        norm_total
        - jnp.mean(norm_total, axis=-1, keepdims=True)
        - own_hat * jnp.mean(norm_total * own_hat, axis=-1, keepdims=True)
    )
    column_sum = jnp.sum(wide_grad, axis=0)
    small_local = jnp.concatenate(
        [
            jnp.sum(grad_one * hat, axis=0),
            jnp.sum(grad_one, axis=0),
            jnp.sum(grad_two * hat, axis=0),
            jnp.sum(grad_two, axis=0),
            jnp.zeros((3 * D,), jnp.float32),
            column_sum,
            jnp.zeros((FF,), jnp.float32),
            column_sum,
        ]
    )
    for k, head in enumerate(heads):
        small_local = lax.dynamic_update_slice_in_dim(
            small_local, bias_parts[0][k * 3 * HD : (k + 1) * 3 * HD], 4 * D + head * 3 * HD, 0
        )
    for k, feeder in enumerate(feeders):
        small_local = lax.dynamic_update_slice_in_dim(
            small_local,
            bias_parts[1][k * feed_wide : (k + 1) * feed_wide],
            8 * D + feeder * feed_wide,
            0,
        )
    small_shard = halve_down(small_local.reshape(count, -1), list(range(bits)), place)[0]
    return (
        layer_out,
        input_grad,
        attend_shard[:head_wide].reshape(-1),
        attend_shard[head_wide:].reshape(-1),
        feed_shard[:feed_wide].reshape(-1),
        feed_shard[feed_wide:].reshape(-1),
        small_shard,
    )


def solution(mesh):
    in_specs = (
        P("fsdp", None),
        P("fsdp", None),
        P("fsdp"),
        P("fsdp"),
        P("fsdp"),
        P("fsdp"),
        P("fsdp"),
        P("fsdp"),
        P("fsdp"),
    )
    out_specs = (
        P("fsdp", None),
        P("fsdp", None),
        P("fsdp"),
        P("fsdp"),
        P("fsdp"),
        P("fsdp"),
        P("fsdp"),
    )
    return jax.shard_map(
        per_device, mesh=mesh, in_specs=in_specs, out_specs=out_specs, check_vma=False
    )
```

```python
import math

import jax
import jax.numpy as jnp
from jax import lax
from jax.sharding import PartitionSpec as P

H = 16
HD = 64
D = 1024
ROT = 16
FF = 4096


norm_epsilon = 1e-05
masked_score = -1e30


def swap(block, mask):
    count = lax.axis_size("fsdp")
    return lax.ppermute(block, "fsdp", [(place, place ^ mask) for place in range(count)])


def left_product(former, latter):
    return lax.dot_general(
        former, latter, (((0,), (0,)), ((), ())), preferred_element_type=jnp.float32
    )


def right_product(former, latter):
    return lax.dot_general(
        former, latter, (((1,), (1,)), ((), ())), preferred_element_type=jnp.float32
    )


def batched(form, former, latter):
    return jnp.einsum(form, former, latter, preferred_element_type=jnp.float32)


def layer_norm(values, gain, shift):
    center = values - jnp.mean(values, axis=-1, keepdims=True)
    spread = jnp.mean(center * center, axis=-1, keepdims=True)
    return center * lax.rsqrt(spread + norm_epsilon) * gain + shift


def rotary_tables(positions):
    halfway = ROT // 2
    powers = jnp.arange(halfway, dtype=jnp.float32) * (2.0 / ROT)
    inverse = 10000.0 ** (-powers)
    angles = positions.astype(jnp.float32)[:, None] * inverse[None, :]
    return (jnp.cos(angles)[:, None, :], jnp.sin(angles)[:, None, :])


def rotate(values, cosine, sine, direction):
    halfway = ROT // 2
    leading = values[..., :halfway]
    trailing = values[..., halfway:ROT]
    new_leading = leading * cosine - direction * trailing * sine
    new_trailing = trailing * cosine + direction * leading * sine
    return jnp.concatenate([new_leading, new_trailing, values[..., ROT:]], axis=-1)


def exact_gelu(values):
    return jax.nn.gelu(values, approximate=False)


def norm_pair(wide_input, norms):
    normed_one = layer_norm(wide_input, norms[0], norms[1]).astype(jnp.bfloat16)
    normed_two = layer_norm(wide_input, norms[2], norms[3]).astype(jnp.bfloat16)
    return (normed_one, normed_two)


def block_scores(query_blocks, key_blocks, label_blocks):
    scale_factor = 1.0 / math.sqrt(HD)
    scores = batched("bqhd,bkhd->bhqk", query_blocks, key_blocks) * scale_factor
    block_rows = label_blocks.shape[1]
    row_order = jnp.arange(block_rows)
    allowed = (label_blocks[:, :, None] == label_blocks[:, None, :]) & (
        row_order[None, None, :] <= row_order[None, :, None]
    )
    return jnp.where(allowed[:, None], scores, masked_score)


def forward_local(normed_one, normed_two, labels, places, weights, blocks):
    attend_rows, attend_bias, output_rows, expand_rows, expand_bias, reduce_rows = weights
    row_count = normed_one.shape[0]
    heads_here = output_rows.shape[0] // HD
    block_rows = row_count // blocks
    projected = right_product(normed_one, attend_rows) + attend_bias
    split = projected.reshape(row_count, heads_here, 3, HD)
    cosine, sine = rotary_tables(places)
    query_heads = (
        rotate(split[:, :, 0], cosine, sine, 1.0)
        .astype(jnp.bfloat16)
        .reshape(blocks, block_rows, heads_here, HD)
    )
    key_heads = (
        rotate(split[:, :, 1], cosine, sine, 1.0)
        .astype(jnp.bfloat16)
        .reshape(blocks, block_rows, heads_here, HD)
    )
    value_heads = split[:, :, 2].astype(jnp.bfloat16).reshape(blocks, block_rows, heads_here, HD)
    label_blocks = labels.reshape(blocks, block_rows)
    scores = block_scores(query_heads, key_heads, label_blocks)
    highest = jnp.max(scores, axis=-1, keepdims=True)
    raised = jnp.exp(scores - highest)
    totals = jnp.sum(raised, axis=-1, keepdims=True)
    soft_low = (raised / totals).astype(jnp.bfloat16)
    log_total = highest + jnp.log(totals)
    mixed_heads = (
        batched("bhqk,bkhd->bqhd", soft_low, value_heads)
        .astype(jnp.bfloat16)
        .reshape(row_count, heads_here * HD)
    )
    expanded = right_product(normed_two, expand_rows) + expand_bias
    activated = exact_gelu(expanded).astype(jnp.bfloat16)
    partial_value = jnp.dot(mixed_heads, output_rows, preferred_element_type=jnp.float32) + jnp.dot(
        activated, reduce_rows, preferred_element_type=jnp.float32
    )
    stored = (
        normed_one,
        normed_two,
        query_heads,
        key_heads,
        value_heads,
        label_blocks,
        log_total,
        mixed_heads,
        expanded,
        activated,
        cosine,
        sine,
    )
    return (partial_value, stored)


def feed_backward(grad_out, grad_activated, stored, weights):
    attend_rows, attend_bias, output_rows, expand_rows, expand_bias, reduce_rows = weights
    (
        normed_one,
        normed_two,
        query_heads,
        key_heads,
        value_heads,
        label_blocks,
        log_total,
        mixed_heads,
        expanded,
        activated,
        cosine,
        sine,
    ) = stored
    grad_reduce = left_product(activated, grad_out)
    pullback = jax.vjp(exact_gelu, expanded)[1]
    grad_expanded = pullback(grad_activated)[0].astype(jnp.bfloat16)
    grad_expand = left_product(grad_expanded, normed_two)
    grad_bias_expand = jnp.sum(grad_expanded.astype(jnp.float32), axis=0)
    grad_normed_two = jnp.dot(grad_expanded, expand_rows, preferred_element_type=jnp.float32)
    return ((grad_expand, grad_reduce), grad_bias_expand, grad_normed_two)


def attend_backward(grad_out, stored, weights):
    attend_rows, attend_bias, output_rows, expand_rows, expand_bias, reduce_rows = weights
    (
        normed_one,
        normed_two,
        query_heads,
        key_heads,
        value_heads,
        label_blocks,
        log_total,
        mixed_heads,
        expanded,
        activated,
        cosine,
        sine,
    ) = stored
    blocks, block_rows, heads_here = (
        query_heads.shape[0],
        query_heads.shape[1],
        query_heads.shape[2],
    )
    row_count = grad_out.shape[0]
    scale_factor = 1.0 / math.sqrt(HD)
    grad_output = left_product(mixed_heads, grad_out)
    grad_mixed = (
        right_product(grad_out, output_rows)
        .astype(jnp.bfloat16)
        .reshape(blocks, block_rows, heads_here, HD)
    )
    scores = block_scores(query_heads, key_heads, label_blocks)
    recomputed = jnp.exp(scores - log_total)
    grad_soft = batched("bqhd,bkhd->bhqk", grad_mixed, value_heads)
    row_inner = jnp.sum(recomputed * grad_soft, axis=-1, keepdims=True)
    grad_scores = (recomputed * (grad_soft - row_inner) * scale_factor).astype(jnp.bfloat16)
    grad_values = batched("bhqk,bqhd->bkhd", recomputed.astype(jnp.bfloat16), grad_mixed)
    grad_queries = rotate(
        batched("bhqk,bkhd->bqhd", grad_scores, key_heads).reshape(row_count, heads_here, HD),
        cosine,
        sine,
        -1.0,
    )
    grad_keys = rotate(
        batched("bhqk,bqhd->bkhd", grad_scores, query_heads).reshape(row_count, heads_here, HD),
        cosine,
        sine,
        -1.0,
    )
    grad_projected = (
        jnp.stack([grad_queries, grad_keys, grad_values.reshape(row_count, heads_here, HD)], axis=2)
        .reshape(row_count, 3 * heads_here * HD)
        .astype(jnp.bfloat16)
    )
    return (grad_projected, grad_output)


def double_up(current, levels, device_place):
    for level in levels:
        theirs = swap(current, 1 << level)
        lower = (device_place >> level) % 2 == 0
        leading = jnp.where(lower, current, theirs)
        trailing = jnp.where(lower, theirs, current)
        current = jnp.concatenate([leading, trailing], axis=0)
    return current


def halve_down(total, levels, device_place):
    for level in reversed(levels):
        middle = total.shape[0] // 2
        lower = (device_place >> level) % 2 == 0
        retained = jnp.where(lower, total[:middle], total[middle:])
        outgoing = jnp.where(lower, total[middle:], total[:middle])
        total = retained + swap(outgoing, 1 << level)
    return total


def gather_pieces(piece, count, shift):
    return [piece] + [swap(piece, k << shift) for k in range(1, count)]


def send_pieces(pieces, shift):
    return [pieces[0]] + [
        swap(pieces[k].astype(jnp.bfloat16), k << shift) for k in range(1, len(pieces))
    ]


def sum_pieces(pieces):
    total = pieces[0].astype(jnp.float32)
    for piece in pieces[1:]:
        total = total + piece.astype(jnp.float32)
    return total


def split_rows(chip):
    rows = chip.shape[0] // 4
    return [chip[k * rows : (k + 1) * rows] for k in range(4)]


def order_low(stacked, bits, place):
    for bit in range(bits):
        shape = stacked.shape
        pairs = stacked.reshape((shape[0] >> (bit + 1), 2, 1 << bit) + shape[1:])
        flipped = jnp.concatenate([pairs[:, 1:], pairs[:, :1]], axis=1)
        stacked = jnp.where((place >> bit) % 2 == 1, flipped, pairs).reshape(shape)
    return stacked


def gather_rows(block, shift):
    mine = jnp.concatenate(gather_pieces(block, 4, shift), axis=0)
    return jnp.concatenate([mine, swap(mine, 1)], axis=0)


def per_device(
    inputs,
    cotangent,
    sequence_ids,
    positions,
    attend_weight,
    output_weight,
    expand_weight,
    reduce_weight,
    small_params,
):
    count = lax.axis_size("fsdp")
    bits = count.bit_length() - 1
    place = lax.axis_index("fsdp")
    token_shift = bits - 2
    chips = count // 8
    core = place % 2
    chip = (place // 2) % chips
    outer = place // (2 * chips)
    per_head = chips // 4
    head_bits = per_head.bit_length() - 1
    row_count = inputs.shape[0]

    head_wide = attend_weight.shape[0] // D
    out_wide = output_weight.shape[0] // D
    feed_wide = expand_weight.shape[0] // D

    labels_all = gather_rows(jnp.stack([sequence_ids, positions], axis=1), token_shift)
    row_pieces = gather_pieces(inputs, 4, token_shift)
    attend_own = jnp.concatenate(
        [attend_weight.reshape(head_wide, D), output_weight.reshape(out_wide, D)], axis=0
    )
    attend_pieces = gather_pieces(attend_own, chips, 1)
    small_all = double_up(small_params[None, :], list(range(bits)), place)
    row_pieces, attend_pieces, small_all, labels_all, cotangent_late, expand_late, reduce_late = (
        lax.optimization_barrier(
            (
                row_pieces,
                attend_pieces,
                small_all,
                labels_all,
                cotangent,
                expand_weight,
                reduce_weight,
            )
        )
    )
    mine = jnp.concatenate(row_pieces, axis=0)
    rows_all = jnp.concatenate([mine, swap(mine, 1)], axis=0)
    attend_half = jnp.stack(attend_pieces)
    low, high = attend_half[: chips // 2], attend_half[chips // 2 :]
    kept = jnp.where(core == 0, low, high)
    theirs = swap(jnp.where(core == 0, high, low), 1)
    first = jnp.where(core == 0, kept, theirs)
    second = jnp.where(core == 0, theirs, kept)
    both = order_low(jnp.stack([first, second], axis=1), head_bits, chip)
    attend_rows = both[:, :, :head_wide].reshape(-1, D)
    output_rows = both[:, :, head_wide:].reshape(-1, D)

    small_wide = small_all.reshape(-1).astype(jnp.float32)
    norms = [small_wide[k * D : (k + 1) * D] for k in range(4)]
    heads = [4 * outer + ((2 * core + k) ^ (chip // per_head)) for k in range(2)]
    attend_bias = jnp.concatenate(
        [lax.dynamic_slice_in_dim(small_wide, 4 * D + head * 3 * HD, 3 * HD) for head in heads]
    )
    feeders = [outer * 2 * chips + (chip ^ k) * 2 + core for k in range(chips)]
    expand_bias = jnp.concatenate(
        [
            lax.dynamic_slice_in_dim(small_wide, 8 * D + feeder * feed_wide, feed_wide)
            for feeder in feeders
        ]
    )
    feed_own = jnp.concatenate(
        [expand_late.reshape(feed_wide, D), reduce_late.reshape(feed_wide, D)], axis=0
    )
    feed_all = jnp.stack(gather_pieces(feed_own, chips, 1))
    expand_rows = feed_all[:, :feed_wide].reshape(-1, D)
    reduce_rows = feed_all[:, feed_wide:].reshape(-1, D)
    weights = (attend_rows, attend_bias, output_rows, expand_rows, expand_bias, reduce_rows)
    grad_rows = gather_rows(cotangent_late, token_shift)

    blocks = 8
    wide_all = rows_all.astype(jnp.float32)
    center = wide_all - jnp.mean(wide_all, axis=-1, keepdims=True)
    inverse = lax.rsqrt(jnp.mean(center * center, axis=-1, keepdims=True) + norm_epsilon)
    hat = center * inverse
    normed_one = (hat * norms[0] + norms[1]).astype(jnp.bfloat16)
    normed_two = (hat * norms[2] + norms[3]).astype(jnp.bfloat16)
    partial_value, stored = forward_local(
        normed_one, normed_two, labels_all[:, 0], labels_all[:, 1], weights, blocks
    )
    half = partial_value.shape[0] // 2
    out_theirs = swap(partial_value[half:].astype(jnp.bfloat16), 1)
    grad_all = jnp.where((labels_all[:, 0] >= 0)[:, None], grad_rows, jnp.zeros_like(grad_rows))
    grad_activated = right_product(grad_all, reduce_rows)
    out_theirs, grad_activated = lax.optimization_barrier((out_theirs, grad_activated))
    out_chip = partial_value[:half] + out_theirs.astype(jnp.float32)
    out_pieces = send_pieces(split_rows(out_chip), token_shift)
    feed_mats, feed_bias, grad_two = feed_backward(grad_all, grad_activated, stored, weights)
    grad_expand, grad_reduce = feed_mats
    feed_pieces = jnp.concatenate(
        [grad_expand.reshape(chips, feed_wide, D), grad_reduce.reshape(chips, feed_wide, D)], axis=1
    )
    feed_low = feed_pieces[1:].astype(jnp.bfloat16)
    feed_low, grad_all, grad_two = lax.optimization_barrier((feed_low, grad_all, grad_two))
    feed_pieces = [feed_pieces[0]] + [
        swap(feed_low[k - 1], k << 1) for k in range(1, chips)
    ]
    grad_projected, grad_output = attend_backward(grad_all, stored, weights)
    grad_one = jnp.dot(grad_projected, attend_rows, preferred_element_type=jnp.float32)
    norm_grad = grad_one * norms[0] + grad_two * norms[2]
    out_pieces, feed_pieces, norm_grad, grad_projected = lax.optimization_barrier(
        (out_pieces, feed_pieces, norm_grad, grad_projected)
    )
    norm_theirs = swap(norm_grad[half:].astype(jnp.bfloat16), 1)
    grad_attend = left_product(grad_projected, normed_one)
    attend_bias_grad = jnp.sum(grad_projected.astype(jnp.float32), axis=0)
    bias_parts = (attend_bias_grad, feed_bias)
    norm_theirs, grad_attend = lax.optimization_barrier((norm_theirs, grad_attend))
    norm_chip = norm_grad[:half] + norm_theirs.astype(jnp.float32)
    norm_pieces = send_pieces(split_rows(norm_chip), token_shift)
    feed_shard = sum_pieces(feed_pieces)
    summed = sum_pieces(out_pieces)
    wide_input = inputs.astype(jnp.float32)
    layer_out = (
        wide_input + summed + small_wide[7 * D : 8 * D] + small_wide[8 * D + FF : 9 * D + FF]
    ).astype(jnp.bfloat16)

    pairs = jnp.concatenate(
        [
            grad_attend.reshape(chips // 2, 2, head_wide, D),
            grad_output.reshape(chips // 2, 2, out_wide, D),
        ],
        axis=2,
    )
    pairs = order_low(pairs, head_bits, chip)
    kept = jnp.where(core == 0, pairs[:, 0], pairs[:, 1])
    theirs = swap(
        jnp.where(core == 0, pairs[:, 1], pairs[:, 0]).astype(jnp.bfloat16), 1
    ).astype(jnp.float32)
    low = jnp.where(core == 0, kept, theirs)
    high = jnp.where(core == 0, theirs, kept)
    halves = [low[k] for k in range(chips // 2)] + [high[k] for k in range(chips // 2)]
    attend_sent = send_pieces(halves, 1)

    grad_out = jnp.where((sequence_ids >= 0)[:, None], cotangent, jnp.zeros_like(cotangent))
    wide_grad = grad_out.astype(jnp.float32)
    column_sum = jnp.sum(wide_grad, axis=0)
    small_local = jnp.concatenate(
        [
            jnp.sum(grad_one * hat, axis=0),
            jnp.sum(grad_one, axis=0),
            jnp.sum(grad_two * hat, axis=0),
            jnp.sum(grad_two, axis=0),
            jnp.zeros((3 * D,), jnp.float32),
            column_sum,
            jnp.zeros((FF,), jnp.float32),
            column_sum,
        ]
    )
    for k, head in enumerate(heads):
        small_local = lax.dynamic_update_slice_in_dim(
            small_local, bias_parts[0][k * 3 * HD : (k + 1) * 3 * HD], 4 * D + head * 3 * HD, 0
        )
    for k, feeder in enumerate(feeders):
        small_local = lax.dynamic_update_slice_in_dim(
            small_local,
            bias_parts[1][k * feed_wide : (k + 1) * feed_wide],
            8 * D + feeder * feed_wide,
            0,
        )
    small_shard = halve_down(small_local.reshape(count, -1), list(range(bits)), place)[0]
    small_shard, attend_sent, norm_pieces = lax.optimization_barrier(
        (small_shard, attend_sent, norm_pieces)
    )
    attend_shard = sum_pieces(attend_sent)
    norm_total = sum_pieces(norm_pieces)
    own_hat = hat[:row_count]
    input_grad = wide_grad + inverse[:row_count] * (
        norm_total
        - jnp.mean(norm_total, axis=-1, keepdims=True)
        - own_hat * jnp.mean(norm_total * own_hat, axis=-1, keepdims=True)
    )
    return (
        layer_out,
        input_grad,
        attend_shard[:head_wide].reshape(-1),
        attend_shard[head_wide:].reshape(-1),
        feed_shard[:feed_wide].reshape(-1),
        feed_shard[feed_wide:].reshape(-1),
        small_shard,
    )


def solution(mesh):
    in_specs = (
        P("fsdp", None),
        P("fsdp", None),
        P("fsdp"),
        P("fsdp"),
        P("fsdp"),
        P("fsdp"),
        P("fsdp"),
        P("fsdp"),
        P("fsdp"),
    )
    out_specs = (
        P("fsdp", None),
        P("fsdp", None),
        P("fsdp"),
        P("fsdp"),
        P("fsdp"),
        P("fsdp"),
        P("fsdp"),
    )
    return jax.shard_map(
        per_device, mesh=mesh, in_specs=in_specs, out_specs=out_specs, check_vma=False
    )
```

```python
import math

import jax
import jax.numpy as jnp
from jax import lax
from jax.sharding import PartitionSpec as P


HD = 64
D = 1024
ROT = 16
FF = 4096


norm_epsilon = 1e-05
masked_score = -1e30


def swap(block, mask):
    count = lax.axis_size("fsdp")
    return lax.ppermute(block, "fsdp", [(place, place ^ mask) for place in range(count)])


def left_product(former, latter):
    return lax.dot_general(
        former, latter, (((0,), (0,)), ((), ())), preferred_element_type=jnp.float32
    )


def right_product(former, latter):
    return lax.dot_general(
        former, latter, (((1,), (1,)), ((), ())), preferred_element_type=jnp.float32
    )


def batched(form, former, latter):
    return jnp.einsum(form, former, latter, preferred_element_type=jnp.float32)


def rotary_tables(positions):
    halfway = ROT // 2
    powers = jnp.arange(halfway, dtype=jnp.float32) * (2.0 / ROT)
    inverse = 10000.0 ** (-powers)
    angles = positions.astype(jnp.float32)[:, None] * inverse[None, :]
    return (jnp.cos(angles)[:, None, :], jnp.sin(angles)[:, None, :])


def rotate(values, cosine, sine, direction):
    halfway = ROT // 2
    leading = values[..., :halfway]
    trailing = values[..., halfway:ROT]
    new_leading = leading * cosine - direction * trailing * sine
    new_trailing = trailing * cosine + direction * leading * sine
    return jnp.concatenate([new_leading, new_trailing, values[..., ROT:]], axis=-1)


def exact_gelu(values):
    return jax.nn.gelu(values, approximate=False)


def block_scores(query_blocks, key_blocks, label_blocks):
    scale_factor = 1.0 / math.sqrt(HD)
    scores = batched("bqhd,bkhd->bhqk", query_blocks, key_blocks) * scale_factor
    block_rows = label_blocks.shape[1]
    row_order = jnp.arange(block_rows)
    allowed = (label_blocks[:, :, None] == label_blocks[:, None, :]) & (
        row_order[None, None, :] <= row_order[None, :, None]
    )
    return jnp.where(allowed[:, None], scores, masked_score)


def forward_local(
    normed_one, normed_two, labels, places, weights, blocks, cotangent_pieces, feed_pieces
):
    attend_rows, attend_bias, output_rows, expand_bias = weights
    row_count = normed_one.shape[0]
    heads_here = output_rows.shape[0] // HD
    block_rows = row_count // blocks
    projected = right_product(normed_one, attend_rows) + attend_bias
    split = projected.reshape(row_count, heads_here, 3, HD)
    cosine, sine = rotary_tables(places)
    query_heads = (
        rotate(split[:, :, 0], cosine, sine, 1.0)
        .astype(jnp.bfloat16)
        .reshape(blocks, block_rows, heads_here, HD)
    )
    key_heads = (
        rotate(split[:, :, 1], cosine, sine, 1.0)
        .astype(jnp.bfloat16)
        .reshape(blocks, block_rows, heads_here, HD)
    )
    value_heads = split[:, :, 2].astype(jnp.bfloat16).reshape(blocks, block_rows, heads_here, HD)
    label_blocks = labels.reshape(blocks, block_rows)
    scores = block_scores(query_heads, key_heads, label_blocks)
    highest = jnp.max(scores, axis=-1, keepdims=True)
    raised = jnp.exp(scores - highest)
    totals = jnp.sum(raised, axis=-1, keepdims=True)
    soft_low = (raised / totals).astype(jnp.bfloat16)
    log_total = highest + jnp.log(totals)
    mixed_heads = (
        batched("bhqk,bkhd->bqhd", soft_low, value_heads)
        .astype(jnp.bfloat16)
        .reshape(row_count, heads_here * HD)
    )
    mixed_heads, cotangent_pieces, feed_pieces = lax.optimization_barrier(
        (mixed_heads, cotangent_pieces, feed_pieces)
    )
    mine = jnp.concatenate(cotangent_pieces, axis=0)
    grad_rows = jnp.concatenate([mine, swap(mine, 1)], axis=0)
    feed_all = jnp.stack(feed_pieces)
    feed_wide = feed_all.shape[1] // 2
    expand_rows = feed_all[:, :feed_wide].reshape(-1, D)
    reduce_rows = feed_all[:, feed_wide:].reshape(-1, D)
    weights = (attend_rows, attend_bias, output_rows, expand_rows, expand_bias, reduce_rows)
    expanded = right_product(normed_two, expand_rows) + expand_bias
    activated = exact_gelu(expanded).astype(jnp.bfloat16)
    partial_value = jnp.dot(mixed_heads, output_rows, preferred_element_type=jnp.float32) + jnp.dot(
        activated, reduce_rows, preferred_element_type=jnp.float32
    )
    stored = (
        normed_one,
        normed_two,
        query_heads,
        key_heads,
        value_heads,
        label_blocks,
        log_total,
        mixed_heads,
        expanded,
        activated,
        cosine,
        sine,
    )
    return (partial_value, stored, weights, grad_rows)


def feed_backward(grad_out, grad_activated, stored, weights):
    _, _, _, expand_rows, _, _ = weights
    (_, normed_two, _, _, _, _, _, _, expanded, activated, _, _) = stored
    grad_reduce = left_product(activated, grad_out)
    pullback = jax.vjp(exact_gelu, expanded)[1]
    grad_expanded = pullback(grad_activated)[0].astype(jnp.bfloat16)
    grad_expand = left_product(grad_expanded, normed_two)
    grad_bias_expand = jnp.sum(grad_expanded.astype(jnp.float32), axis=0)
    grad_normed_two = jnp.dot(grad_expanded, expand_rows, preferred_element_type=jnp.float32)
    return ((grad_expand, grad_reduce), grad_bias_expand, grad_normed_two)


def attend_backward(grad_out, stored, weights):
    _, _, output_rows, _, _, _ = weights
    (
        _,
        _,
        query_heads,
        key_heads,
        value_heads,
        label_blocks,
        log_total,
        mixed_heads,
        _,
        _,
        cosine,
        sine,
    ) = stored
    blocks, block_rows, heads_here = (
        query_heads.shape[0],
        query_heads.shape[1],
        query_heads.shape[2],
    )
    row_count = grad_out.shape[0]
    scale_factor = 1.0 / math.sqrt(HD)
    grad_output = left_product(mixed_heads, grad_out)
    grad_mixed = (
        right_product(grad_out, output_rows)
        .astype(jnp.bfloat16)
        .reshape(blocks, block_rows, heads_here, HD)
    )
    scores = block_scores(query_heads, key_heads, label_blocks)
    recomputed = jnp.exp(scores - log_total)
    grad_soft = batched("bqhd,bkhd->bhqk", grad_mixed, value_heads)
    row_inner = jnp.sum(recomputed * grad_soft, axis=-1, keepdims=True)
    grad_scores = (recomputed * (grad_soft - row_inner) * scale_factor).astype(jnp.bfloat16)
    grad_values = batched("bhqk,bqhd->bkhd", recomputed.astype(jnp.bfloat16), grad_mixed)
    grad_queries = rotate(
        batched("bhqk,bkhd->bqhd", grad_scores, key_heads).reshape(row_count, heads_here, HD),
        cosine,
        sine,
        -1.0,
    )
    grad_keys = rotate(
        batched("bhqk,bqhd->bkhd", grad_scores, query_heads).reshape(row_count, heads_here, HD),
        cosine,
        sine,
        -1.0,
    )
    grad_projected = (
        jnp.stack([grad_queries, grad_keys, grad_values.reshape(row_count, heads_here, HD)], axis=2)
        .reshape(row_count, 3 * heads_here * HD)
        .astype(jnp.bfloat16)
    )
    return (grad_projected, grad_output)


def double_up(current, levels, device_place):
    for level in levels:
        theirs = swap(current, 1 << level)
        lower = (device_place >> level) % 2 == 0
        leading = jnp.where(lower, current, theirs)
        trailing = jnp.where(lower, theirs, current)
        current = jnp.concatenate([leading, trailing], axis=0)
    return current


def halve_down(total, levels, device_place):
    for level in reversed(levels):
        middle = total.shape[0] // 2
        lower = (device_place >> level) % 2 == 0
        retained = jnp.where(lower, total[:middle], total[middle:])
        outgoing = jnp.where(lower, total[middle:], total[:middle])
        total = retained + swap(outgoing, 1 << level)
    return total


def gather_pieces(piece, count, shift):
    return [piece] + [swap(piece, k << shift) for k in range(1, count)]


def send_pieces(pieces, shift):
    return [pieces[0]] + [
        swap(pieces[k].astype(jnp.bfloat16), k << shift)
        for k in range(1, len(pieces))
    ]


def sum_pieces(pieces):
    total = pieces[0].astype(jnp.float32)
    for piece in pieces[1:]:
        total = total + piece.astype(jnp.float32)
    return total


def split_rows(chip):
    rows = chip.shape[0] // 4
    return [chip[k * rows : (k + 1) * rows] for k in range(4)]


def order_low(stacked, bits, place):
    for bit in range(bits):
        shape = stacked.shape
        pairs = stacked.reshape((shape[0] >> (bit + 1), 2, 1 << bit) + shape[1:])
        flipped = jnp.concatenate([pairs[:, 1:], pairs[:, :1]], axis=1)
        stacked = jnp.where((place >> bit) % 2 == 1, flipped, pairs).reshape(shape)
    return stacked


def per_device(
    inputs,
    cotangent,
    sequence_ids,
    positions,
    attend_weight,
    output_weight,
    expand_weight,
    reduce_weight,
    small_params,
):
    count = lax.axis_size("fsdp")
    bits = count.bit_length() - 1
    place = lax.axis_index("fsdp")
    token_shift = bits - 2
    chips = count // 8
    core = place % 2
    chip = (place // 2) % chips
    outer = place // (2 * chips)
    per_head = chips // 4
    head_bits = per_head.bit_length() - 1
    row_count = inputs.shape[0]

    head_wide = attend_weight.shape[0] // D
    out_wide = output_weight.shape[0] // D
    feed_wide = expand_weight.shape[0] // D

    shifted = sequence_ids + 1
    digits = jnp.concatenate([shifted // 256, shifted % 256, positions // 256, positions % 256])
    packet = jnp.concatenate([small_params, digits.astype(jnp.bfloat16)])[None, :]
    small_wide_own = small_params.shape[0]
    row_pieces = gather_pieces(inputs, 4, token_shift)
    attend_own = jnp.concatenate(
        [attend_weight.reshape(head_wide, D), output_weight.reshape(out_wide, D)], axis=0
    )
    attend_pieces = gather_pieces(attend_own, chips, 1)
    small_all = double_up(packet, list(range(bits)), place)
    row_pieces, attend_pieces, small_all, cotangent_late, expand_late, reduce_late = (
        lax.optimization_barrier(
            (
                row_pieces,
                attend_pieces,
                small_all,
                cotangent,
                expand_weight,
                reduce_weight,
            )
        )
    )
    mine = jnp.concatenate(row_pieces, axis=0)
    rows_all = jnp.concatenate([mine, swap(mine, 1)], axis=0)
    attend_half = jnp.stack(attend_pieces)
    low, high = attend_half[: chips // 2], attend_half[chips // 2 :]
    kept = jnp.where(core == 0, low, high)
    theirs = swap(jnp.where(core == 0, high, low), 1)
    first = jnp.where(core == 0, kept, theirs)
    second = jnp.where(core == 0, theirs, kept)
    both = order_low(jnp.stack([first, second], axis=1), head_bits, chip)
    attend_rows = both[:, :, :head_wide].reshape(-1, D)
    output_rows = both[:, :, head_wide:].reshape(-1, D)

    small_wide = small_all[:, :small_wide_own].reshape(-1).astype(jnp.float32)
    labels_every = small_all[:, small_wide_own:].reshape(4, chips, 2, -1)
    labels_here = lax.dynamic_index_in_dim(labels_every, chip, 1, keepdims=False)
    labels_here = labels_here.transpose(1, 0, 2).reshape(8, -1).astype(jnp.float32)
    labels_here = order_low(labels_here, 3, core * 4 + outer).reshape(8, 4, row_count)
    labels_all = (labels_here[:, 0] * 256 + labels_here[:, 1]).astype(jnp.int32).reshape(-1) - 1
    places_all = (labels_here[:, 2] * 256 + labels_here[:, 3]).astype(jnp.int32).reshape(-1)
    norms = [small_wide[k * D : (k + 1) * D] for k in range(4)]
    heads = [4 * outer + ((2 * core + k) ^ (chip // per_head)) for k in range(2)]
    attend_bias = jnp.concatenate(
        [lax.dynamic_slice_in_dim(small_wide, 4 * D + head * 3 * HD, 3 * HD) for head in heads]
    )
    feeders = [outer * 2 * chips + (chip ^ k) * 2 + core for k in range(chips)]
    expand_bias = jnp.concatenate(
        [
            lax.dynamic_slice_in_dim(small_wide, 8 * D + feeder * feed_wide, feed_wide)
            for feeder in feeders
        ]
    )
    feed_own = jnp.concatenate(
        [expand_late.reshape(feed_wide, D), reduce_late.reshape(feed_wide, D)], axis=0
    )
    feed_pieces = gather_pieces(feed_own, chips, 1)
    weights = (attend_rows, attend_bias, output_rows, expand_bias)
    cotangent_pieces = gather_pieces(cotangent_late, 4, token_shift)

    blocks = 8
    wide_all = rows_all.astype(jnp.float32)
    center = wide_all - jnp.mean(wide_all, axis=-1, keepdims=True)
    inverse = lax.rsqrt(jnp.mean(center * center, axis=-1, keepdims=True) + norm_epsilon)
    hat = center * inverse
    normed_one = (hat * norms[0] + norms[1]).astype(jnp.bfloat16)
    normed_two = (hat * norms[2] + norms[3]).astype(jnp.bfloat16)
    partial_value, stored, weights, grad_rows = forward_local(
        normed_one,
        normed_two,
        labels_all,
        places_all,
        weights,
        blocks,
        cotangent_pieces,
        feed_pieces,
    )
    reduce_rows = weights[5]
    half = partial_value.shape[0] // 2
    out_theirs = swap(partial_value[half:].astype(jnp.bfloat16), 1)
    grad_all = jnp.where((labels_all >= 0)[:, None], grad_rows, jnp.zeros_like(grad_rows))
    grad_activated = right_product(grad_all, reduce_rows)
    out_theirs, grad_activated = lax.optimization_barrier((out_theirs, grad_activated))
    out_chip = partial_value[:half] + out_theirs.astype(jnp.float32)
    out_pieces = send_pieces(split_rows(out_chip), token_shift)
    feed_mats, feed_bias, grad_two = feed_backward(grad_all, grad_activated, stored, weights)
    grad_expand, grad_reduce = feed_mats
    feed_pieces = jnp.concatenate(
        [grad_expand.reshape(chips, feed_wide, D), grad_reduce.reshape(chips, feed_wide, D)], axis=1
    )
    feed_low = feed_pieces[1:].astype(jnp.bfloat16)
    feed_low, grad_all, grad_two = lax.optimization_barrier((feed_low, grad_all, grad_two))
    feed_pieces = [feed_pieces[0]] + [swap(feed_low[k - 1], k << 1) for k in range(1, chips)]
    grad_projected, grad_output = attend_backward(grad_all, stored, weights)
    grad_one = jnp.dot(grad_projected, attend_rows, preferred_element_type=jnp.float32)
    norm_grad = grad_one * norms[0] + grad_two * norms[2]
    out_pieces, feed_pieces, norm_grad, grad_projected = lax.optimization_barrier(
        (out_pieces, feed_pieces, norm_grad, grad_projected)
    )
    norm_theirs = swap(norm_grad[half:].astype(jnp.bfloat16), 1)
    grad_attend = left_product(grad_projected, normed_one)
    attend_bias_grad = jnp.sum(grad_projected.astype(jnp.float32), axis=0)
    bias_parts = (attend_bias_grad, feed_bias)
    norm_theirs, grad_attend = lax.optimization_barrier((norm_theirs, grad_attend))
    norm_chip = norm_grad[:half] + norm_theirs.astype(jnp.float32)
    norm_pieces = send_pieces(split_rows(norm_chip), token_shift)
    feed_shard = sum_pieces(feed_pieces)
    summed = sum_pieces(out_pieces)
    wide_input = inputs.astype(jnp.float32)
    layer_out = (
        wide_input + summed + small_wide[7 * D : 8 * D] + small_wide[8 * D + FF : 9 * D + FF]
    ).astype(jnp.bfloat16)

    pairs = jnp.concatenate(
        [
            grad_attend.reshape(chips // 2, 2, head_wide, D),
            grad_output.reshape(chips // 2, 2, out_wide, D),
        ],
        axis=2,
    )
    pairs = order_low(pairs, head_bits, chip)
    kept = jnp.where(core == 0, pairs[:, 0], pairs[:, 1])
    theirs = swap(
        jnp.where(core == 0, pairs[:, 1], pairs[:, 0]).astype(jnp.bfloat16), 1
    ).astype(jnp.float32)
    low = jnp.where(core == 0, kept, theirs)
    high = jnp.where(core == 0, theirs, kept)
    halves = [low[k] for k in range(chips // 2)] + [high[k] for k in range(chips // 2)]
    attend_sent = send_pieces(halves, 1)

    grad_out = jnp.where((sequence_ids >= 0)[:, None], cotangent, jnp.zeros_like(cotangent))
    wide_grad = grad_out.astype(jnp.float32)
    column_sum = jnp.sum(wide_grad, axis=0)
    small_local = jnp.concatenate(
        [
            jnp.sum(grad_one * hat, axis=0),
            jnp.sum(grad_one, axis=0),
            jnp.sum(grad_two * hat, axis=0),
            jnp.sum(grad_two, axis=0),
            jnp.zeros((3 * D,), jnp.float32),
            column_sum,
            jnp.zeros((FF,), jnp.float32),
            column_sum,
        ]
    )
    for k, head in enumerate(heads):
        small_local = lax.dynamic_update_slice_in_dim(
            small_local, bias_parts[0][k * 3 * HD : (k + 1) * 3 * HD], 4 * D + head * 3 * HD, 0
        )
    for k, feeder in enumerate(feeders):
        small_local = lax.dynamic_update_slice_in_dim(
            small_local,
            bias_parts[1][k * feed_wide : (k + 1) * feed_wide],
            8 * D + feeder * feed_wide,
            0,
        )
    small_shard = halve_down(small_local.reshape(count, -1), list(range(bits)), place)[0]
    small_shard, attend_sent, norm_pieces = lax.optimization_barrier(
        (small_shard, attend_sent, norm_pieces)
    )
    attend_shard = sum_pieces(attend_sent)
    norm_total = sum_pieces(norm_pieces)
    own_hat = hat[:row_count]
    input_grad = wide_grad + inverse[:row_count] * (
        norm_total
        - jnp.mean(norm_total, axis=-1, keepdims=True)
        - own_hat * jnp.mean(norm_total * own_hat, axis=-1, keepdims=True)
    )
    return (
        layer_out,
        input_grad,
        attend_shard[:head_wide].reshape(-1),
        attend_shard[head_wide:].reshape(-1),
        feed_shard[:feed_wide].reshape(-1),
        feed_shard[feed_wide:].reshape(-1),
        small_shard,
    )


def solution(mesh):
    in_specs = (
        P("fsdp", None),
        P("fsdp", None),
        P("fsdp"),
        P("fsdp"),
        P("fsdp"),
        P("fsdp"),
        P("fsdp"),
        P("fsdp"),
        P("fsdp"),
    )
    out_specs = (
        P("fsdp", None),
        P("fsdp", None),
        P("fsdp"),
        P("fsdp"),
        P("fsdp"),
        P("fsdp"),
        P("fsdp"),
    )
    return jax.shard_map(
        per_device, mesh=mesh, in_specs=in_specs, out_specs=out_specs, check_vma=False
    )
```

```python
import math

import jax
import jax.numpy as jnp
from jax import lax
from jax.sharding import PartitionSpec as P


HD = 64
D = 1024
ROT = 16
FF = 4096


norm_epsilon = 1e-05
masked_score = -1e30


def swap(block, mask):
    count = lax.axis_size("fsdp")
    return lax.ppermute(block, "fsdp", [(place, place ^ mask) for place in range(count)])


def left_product(former, latter):
    return lax.dot_general(
        former, latter, (((0,), (0,)), ((), ())), preferred_element_type=jnp.float32
    )


def right_product(former, latter):
    return lax.dot_general(
        former, latter, (((1,), (1,)), ((), ())), preferred_element_type=jnp.float32
    )


def batched(form, former, latter):
    return jnp.einsum(form, former, latter, preferred_element_type=jnp.float32)


def rotary_tables(positions):
    halfway = ROT // 2
    powers = jnp.arange(halfway, dtype=jnp.float32) * (2.0 / ROT)
    inverse = 10000.0 ** (-powers)
    angles = positions.astype(jnp.float32)[:, None] * inverse[None, :]
    return (jnp.cos(angles)[:, None, :], jnp.sin(angles)[:, None, :])


def rotate(values, cosine, sine, direction):
    halfway = ROT // 2
    leading = values[..., :halfway]
    trailing = values[..., halfway:ROT]
    new_leading = leading * cosine - direction * trailing * sine
    new_trailing = trailing * cosine + direction * leading * sine
    return jnp.concatenate([new_leading, new_trailing, values[..., ROT:]], axis=-1)


def exact_gelu(values):
    return jax.nn.gelu(values, approximate=False)


def block_scores(query_blocks, key_blocks, label_blocks):
    scale_factor = 1.0 / math.sqrt(HD)
    scores = batched("bqhd,bkhd->bhqk", query_blocks, key_blocks) * scale_factor
    block_rows = label_blocks.shape[1]
    row_order = jnp.arange(block_rows)
    allowed = (label_blocks[:, :, None] == label_blocks[:, None, :]) & (
        row_order[None, None, :] <= row_order[None, :, None]
    )
    return jnp.where(allowed[:, None], scores, masked_score)


def forward_local(
    normed_one, normed_two, labels, places, weights, blocks, cotangent_pieces, feed_pieces
):
    attend_rows, attend_bias, output_rows, expand_bias = weights
    row_count = normed_one.shape[0]
    heads_here = output_rows.shape[0] // HD
    block_rows = row_count // blocks
    projected = right_product(normed_one, attend_rows) + attend_bias
    split = projected.reshape(row_count, heads_here, 3, HD)
    cosine, sine = rotary_tables(places)
    query_heads = (
        rotate(split[:, :, 0], cosine, sine, 1.0)
        .astype(jnp.bfloat16)
        .reshape(blocks, block_rows, heads_here, HD)
    )
    key_heads = (
        rotate(split[:, :, 1], cosine, sine, 1.0)
        .astype(jnp.bfloat16)
        .reshape(blocks, block_rows, heads_here, HD)
    )
    value_heads = split[:, :, 2].astype(jnp.bfloat16).reshape(blocks, block_rows, heads_here, HD)
    label_blocks = labels.reshape(blocks, block_rows)
    scores = block_scores(query_heads, key_heads, label_blocks)
    highest = jnp.max(scores, axis=-1, keepdims=True)
    raised = jnp.exp(scores - highest)
    totals = jnp.sum(raised, axis=-1, keepdims=True)
    soft_low = (raised / totals).astype(jnp.bfloat16)
    log_total = highest + jnp.log(totals)
    mixed_heads = (
        batched("bhqk,bkhd->bqhd", soft_low, value_heads)
        .astype(jnp.bfloat16)
        .reshape(row_count, heads_here * HD)
    )
    mixed_heads, cotangent_pieces, feed_pieces = lax.optimization_barrier(
        (mixed_heads, cotangent_pieces, feed_pieces)
    )
    mine = jnp.concatenate(cotangent_pieces, axis=0)
    grad_rows = jnp.concatenate([mine, swap(mine, 1)], axis=0)
    feed_all = jnp.stack(feed_pieces)
    feed_wide = feed_all.shape[1] // 2
    expand_rows = feed_all[:, :feed_wide].reshape(-1, D)
    reduce_rows = feed_all[:, feed_wide:].reshape(-1, D)
    weights = (attend_rows, attend_bias, output_rows, expand_rows, expand_bias, reduce_rows)
    expanded = right_product(normed_two, expand_rows) + expand_bias
    activated = exact_gelu(expanded).astype(jnp.bfloat16)
    partial_value = jnp.dot(mixed_heads, output_rows, preferred_element_type=jnp.float32) + jnp.dot(
        activated, reduce_rows, preferred_element_type=jnp.float32
    )
    stored = (
        normed_one,
        normed_two,
        query_heads,
        key_heads,
        value_heads,
        label_blocks,
        log_total,
        mixed_heads,
        expanded,
        activated,
        cosine,
        sine,
    )
    return (partial_value, stored, weights, grad_rows)


def feed_backward(grad_out, grad_activated, stored, weights):
    _, _, _, expand_rows, _, _ = weights
    (_, normed_two, _, _, _, _, _, _, expanded, activated, _, _) = stored
    grad_reduce = left_product(activated, grad_out)
    pullback = jax.vjp(exact_gelu, expanded)[1]
    grad_expanded = pullback(grad_activated)[0].astype(jnp.bfloat16)
    grad_expand = left_product(grad_expanded, normed_two)
    grad_bias_expand = jnp.sum(grad_expanded.astype(jnp.float32), axis=0)
    grad_normed_two = jnp.dot(grad_expanded, expand_rows, preferred_element_type=jnp.float32)
    return ((grad_expand, grad_reduce), grad_bias_expand, grad_normed_two)


def attend_backward(grad_out, stored, weights):
    _, _, output_rows, _, _, _ = weights
    (
        _,
        _,
        query_heads,
        key_heads,
        value_heads,
        label_blocks,
        log_total,
        mixed_heads,
        _,
        _,
        cosine,
        sine,
    ) = stored
    blocks, block_rows, heads_here = (
        query_heads.shape[0],
        query_heads.shape[1],
        query_heads.shape[2],
    )
    row_count = grad_out.shape[0]
    scale_factor = 1.0 / math.sqrt(HD)
    grad_output = left_product(mixed_heads, grad_out)
    grad_mixed = (
        right_product(grad_out, output_rows)
        .astype(jnp.bfloat16)
        .reshape(blocks, block_rows, heads_here, HD)
    )
    scores = block_scores(query_heads, key_heads, label_blocks)
    recomputed = jnp.exp(scores - log_total)
    grad_soft = batched("bqhd,bkhd->bhqk", grad_mixed, value_heads)
    row_inner = jnp.sum(recomputed * grad_soft, axis=-1, keepdims=True)
    grad_scores = (recomputed * (grad_soft - row_inner) * scale_factor).astype(jnp.bfloat16)
    grad_values = batched("bhqk,bqhd->bkhd", recomputed.astype(jnp.bfloat16), grad_mixed)
    grad_queries = rotate(
        batched("bhqk,bkhd->bqhd", grad_scores, key_heads).reshape(row_count, heads_here, HD),
        cosine,
        sine,
        -1.0,
    )
    grad_keys = rotate(
        batched("bhqk,bqhd->bkhd", grad_scores, query_heads).reshape(row_count, heads_here, HD),
        cosine,
        sine,
        -1.0,
    )
    grad_projected = (
        jnp.stack([grad_queries, grad_keys, grad_values.reshape(row_count, heads_here, HD)], axis=2)
        .reshape(row_count, 3 * heads_here * HD)
        .astype(jnp.bfloat16)
    )
    return (grad_projected, grad_output)


def halve_axis(total, axis, mask, lower):
    leading, trailing = jnp.split(total, 2, axis=axis)
    retained = jnp.where(lower, leading, trailing)
    return retained + swap(jnp.where(lower, trailing, leading), mask)


def double_axis(current, axis, mask, lower):
    theirs = swap(current, mask)
    leading = jnp.where(lower, current, theirs)
    trailing = jnp.where(lower, theirs, current)
    return jnp.concatenate([leading, trailing], axis=axis)


def gather_pieces(piece, count, shift):
    return [piece] + [swap(piece, k << shift) for k in range(1, count)]


def send_pieces(pieces, shift):
    return [pieces[0]] + [
        swap(pieces[k].astype(jnp.bfloat16), k << shift)
        for k in range(1, len(pieces))
    ]


def sum_pieces(pieces):
    total = pieces[0].astype(jnp.float32)
    for piece in pieces[1:]:
        total = total + piece.astype(jnp.float32)
    return total


def split_rows(chip):
    rows = chip.shape[0] // 4
    return [chip[k * rows : (k + 1) * rows] for k in range(4)]


def order_low(stacked, bits, place):
    for bit in range(bits):
        shape = stacked.shape
        pairs = stacked.reshape((shape[0] >> (bit + 1), 2, 1 << bit) + shape[1:])
        flipped = jnp.concatenate([pairs[:, 1:], pairs[:, :1]], axis=1)
        stacked = jnp.where((place >> bit) % 2 == 1, flipped, pairs).reshape(shape)
    return stacked


def per_device(
    inputs,
    cotangent,
    sequence_ids,
    positions,
    attend_weight,
    output_weight,
    expand_weight,
    reduce_weight,
    small_params,
):
    count = lax.axis_size("fsdp")
    bits = count.bit_length() - 1
    place = lax.axis_index("fsdp")
    token_shift = bits - 2
    chips = count // 8
    core = place % 2
    chip = (place // 2) % chips
    outer = place // (2 * chips)
    per_head = chips // 4
    head_bits = per_head.bit_length() - 1
    row_count = inputs.shape[0]

    head_wide = attend_weight.shape[0] // D
    out_wide = output_weight.shape[0] // D
    feed_wide = expand_weight.shape[0] // D

    shifted = sequence_ids + 1
    digits = jnp.concatenate([shifted // 256, shifted % 256, positions // 256, positions % 256])
    packet = jnp.concatenate([small_params, digits.astype(jnp.bfloat16)])[None, :]
    small_wide_own = small_params.shape[0]
    row_pieces = gather_pieces(inputs, 4, token_shift)
    attend_own = jnp.concatenate(
        [attend_weight.reshape(head_wide, D), output_weight.reshape(out_wide, D)], axis=0
    )
    attend_pieces = gather_pieces(attend_own, chips, 1)
    outer_all = jnp.concatenate(gather_pieces(packet, 4, token_shift), axis=0)
    outer_all = order_low(outer_all, 2, outer)[:, None]
    small_all = double_axis(outer_all, 1, 1, core == 0)[:, None]
    chip_bits = chips.bit_length() - 1
    for bit in range(chip_bits):
        small_all = double_axis(small_all, 1, 2 << bit, (chip >> bit) % 2 == 0)
    row_pieces, attend_pieces, small_all, cotangent_late, expand_late, reduce_late = (
        lax.optimization_barrier(
            (
                row_pieces,
                attend_pieces,
                small_all,
                cotangent,
                expand_weight,
                reduce_weight,
            )
        )
    )
    mine = jnp.concatenate(row_pieces, axis=0)
    rows_all = jnp.concatenate([mine, swap(mine, 1)], axis=0)
    attend_half = jnp.stack(attend_pieces)
    low, high = attend_half[: chips // 2], attend_half[chips // 2 :]
    kept = jnp.where(core == 0, low, high)
    theirs = swap(jnp.where(core == 0, high, low), 1)
    first = jnp.where(core == 0, kept, theirs)
    second = jnp.where(core == 0, theirs, kept)
    both = order_low(jnp.stack([first, second], axis=1), head_bits, chip)
    attend_rows = both[:, :, :head_wide].reshape(-1, D)
    output_rows = both[:, :, head_wide:].reshape(-1, D)

    small_wide = small_all[..., :small_wide_own].reshape(-1).astype(jnp.float32)
    labels_every = small_all[..., small_wide_own:]
    labels_here = lax.dynamic_index_in_dim(labels_every, chip, 1, keepdims=False)
    labels_here = labels_here.transpose(1, 0, 2).reshape(8, -1).astype(jnp.float32)
    labels_here = order_low(labels_here, 3, core * 4 + outer).reshape(8, 4, row_count)
    labels_all = (labels_here[:, 0] * 256 + labels_here[:, 1]).astype(jnp.int32).reshape(-1) - 1
    places_all = (labels_here[:, 2] * 256 + labels_here[:, 3]).astype(jnp.int32).reshape(-1)
    norms = [small_wide[k * D : (k + 1) * D] for k in range(4)]
    heads = [4 * outer + ((2 * core + k) ^ (chip // per_head)) for k in range(2)]
    attend_bias = jnp.concatenate(
        [lax.dynamic_slice_in_dim(small_wide, 4 * D + head * 3 * HD, 3 * HD) for head in heads]
    )
    feeders = [outer * 2 * chips + (chip ^ k) * 2 + core for k in range(chips)]
    expand_bias = jnp.concatenate(
        [
            lax.dynamic_slice_in_dim(small_wide, 8 * D + feeder * feed_wide, feed_wide)
            for feeder in feeders
        ]
    )
    feed_own = jnp.concatenate(
        [expand_late.reshape(feed_wide, D), reduce_late.reshape(feed_wide, D)], axis=0
    )
    feed_pieces = gather_pieces(feed_own, chips, 1)
    weights = (attend_rows, attend_bias, output_rows, expand_bias)
    cotangent_pieces = gather_pieces(cotangent_late, 4, token_shift)

    blocks = 8
    wide_all = rows_all.astype(jnp.float32)
    center = wide_all - jnp.mean(wide_all, axis=-1, keepdims=True)
    inverse = lax.rsqrt(jnp.mean(center * center, axis=-1, keepdims=True) + norm_epsilon)
    hat = center * inverse
    normed_one = (hat * norms[0] + norms[1]).astype(jnp.bfloat16)
    normed_two = (hat * norms[2] + norms[3]).astype(jnp.bfloat16)
    partial_value, stored, weights, grad_rows = forward_local(
        normed_one,
        normed_two,
        labels_all,
        places_all,
        weights,
        blocks,
        cotangent_pieces,
        feed_pieces,
    )
    reduce_rows = weights[5]
    half = partial_value.shape[0] // 2
    out_theirs = swap(partial_value[half:].astype(jnp.bfloat16), 1)
    grad_all = jnp.where((labels_all >= 0)[:, None], grad_rows, jnp.zeros_like(grad_rows))
    grad_activated = right_product(grad_all, reduce_rows)
    out_theirs, grad_activated = lax.optimization_barrier((out_theirs, grad_activated))
    out_chip = partial_value[:half] + out_theirs.astype(jnp.float32)
    out_pieces = send_pieces(split_rows(out_chip), token_shift)
    feed_mats, feed_bias, grad_two = feed_backward(grad_all, grad_activated, stored, weights)
    grad_expand, grad_reduce = feed_mats
    feed_pieces = jnp.concatenate(
        [grad_expand.reshape(chips, feed_wide, D), grad_reduce.reshape(chips, feed_wide, D)], axis=1
    )
    feed_low = feed_pieces[1:].astype(jnp.bfloat16)
    feed_low, grad_all, grad_two = lax.optimization_barrier((feed_low, grad_all, grad_two))
    feed_pieces = [feed_pieces[0]] + [swap(feed_low[k - 1], k << 1) for k in range(1, chips)]
    grad_projected, grad_output = attend_backward(grad_all, stored, weights)
    grad_one = jnp.dot(grad_projected, attend_rows, preferred_element_type=jnp.float32)
    norm_grad = grad_one * norms[0] + grad_two * norms[2]
    out_pieces, feed_pieces, norm_grad, grad_projected = lax.optimization_barrier(
        (out_pieces, feed_pieces, norm_grad, grad_projected)
    )
    norm_theirs = swap(norm_grad[half:].astype(jnp.bfloat16), 1)
    grad_attend = left_product(grad_projected, normed_one)
    attend_bias_grad = jnp.sum(grad_projected.astype(jnp.float32), axis=0)
    bias_parts = (attend_bias_grad, feed_bias)
    norm_theirs, grad_attend = lax.optimization_barrier((norm_theirs, grad_attend))
    norm_chip = norm_grad[:half] + norm_theirs.astype(jnp.float32)
    norm_pieces = send_pieces(split_rows(norm_chip), token_shift)
    feed_shard = sum_pieces(feed_pieces)
    summed = sum_pieces(out_pieces)
    wide_input = inputs.astype(jnp.float32)
    layer_out = (
        wide_input + summed + small_wide[7 * D : 8 * D] + small_wide[8 * D + FF : 9 * D + FF]
    ).astype(jnp.bfloat16)

    pairs = jnp.concatenate(
        [
            grad_attend.reshape(chips // 2, 2, head_wide, D),
            grad_output.reshape(chips // 2, 2, out_wide, D),
        ],
        axis=2,
    )
    pairs = order_low(pairs, head_bits, chip)
    kept = jnp.where(core == 0, pairs[:, 0], pairs[:, 1])
    theirs = swap(
        jnp.where(core == 0, pairs[:, 1], pairs[:, 0]).astype(jnp.bfloat16), 1
    ).astype(jnp.float32)
    low = jnp.where(core == 0, kept, theirs)
    high = jnp.where(core == 0, theirs, kept)
    halves = [low[k] for k in range(chips // 2)] + [high[k] for k in range(chips // 2)]
    attend_sent = send_pieces(halves, 1)

    grad_out = jnp.where((sequence_ids >= 0)[:, None], cotangent, jnp.zeros_like(cotangent))
    wide_grad = grad_out.astype(jnp.float32)
    column_sum = jnp.sum(wide_grad, axis=0)
    small_local = jnp.concatenate(
        [
            jnp.sum(grad_one * hat, axis=0),
            jnp.sum(grad_one, axis=0),
            jnp.sum(grad_two * hat, axis=0),
            jnp.sum(grad_two, axis=0),
            jnp.zeros((3 * D,), jnp.float32),
            column_sum,
            jnp.zeros((FF,), jnp.float32),
            column_sum,
        ]
    )
    for k, head in enumerate(heads):
        small_local = lax.dynamic_update_slice_in_dim(
            small_local, bias_parts[0][k * 3 * HD : (k + 1) * 3 * HD], 4 * D + head * 3 * HD, 0
        )
    for k, feeder in enumerate(feeders):
        small_local = lax.dynamic_update_slice_in_dim(
            small_local,
            bias_parts[1][k * feed_wide : (k + 1) * feed_wide],
            8 * D + feeder * feed_wide,
            0,
        )
    small_part = small_local.reshape(4, chips, 2, -1)
    small_part = halve_axis(small_part, 2, 1, core == 0)
    for bit in reversed(range(chip_bits)):
        small_part = halve_axis(small_part, 1, 2 << bit, (chip >> bit) % 2 == 0)
    small_part = order_low(small_part.reshape(4, -1), 2, outer)
    small_sent = [small_part[0]] + [swap(small_part[k], k << token_shift) for k in range(1, 4)]
    small_sent, attend_sent, norm_pieces = lax.optimization_barrier(
        (small_sent, attend_sent, norm_pieces)
    )
    small_shard = sum_pieces(small_sent)
    attend_shard = sum_pieces(attend_sent)
    norm_total = sum_pieces(norm_pieces)
    own_hat = hat[:row_count]
    input_grad = wide_grad + inverse[:row_count] * (
        norm_total
        - jnp.mean(norm_total, axis=-1, keepdims=True)
        - own_hat * jnp.mean(norm_total * own_hat, axis=-1, keepdims=True)
    )
    return (
        layer_out,
        input_grad,
        attend_shard[:head_wide].reshape(-1),
        attend_shard[head_wide:].reshape(-1),
        feed_shard[:feed_wide].reshape(-1),
        feed_shard[feed_wide:].reshape(-1),
        small_shard,
    )


def solution(mesh):
    in_specs = (
        P("fsdp", None),
        P("fsdp", None),
        P("fsdp"),
        P("fsdp"),
        P("fsdp"),
        P("fsdp"),
        P("fsdp"),
        P("fsdp"),
        P("fsdp"),
    )
    out_specs = (
        P("fsdp", None),
        P("fsdp", None),
        P("fsdp"),
        P("fsdp"),
        P("fsdp"),
        P("fsdp"),
        P("fsdp"),
    )
    return jax.shard_map(
        per_device, mesh=mesh, in_specs=in_specs, out_specs=out_specs, check_vma=False
    )
```
